32 devices in a mesh: axial: 16 (over z, y, core), trans: 2 (over x).
Axes of the slice: x: 2, y: 2, z: 4, core: 2. Of those that a mesh axis runs over, the one named last changes fastest.
Arguments:
- source: float32 [128, 512, 512], P('axial', 'trans'), may hold values from -6 to 6
- labels: int32 [128, 512, 512], P('axial', 'trans'), may hold values from 0 to 3
- voltages: float32 [4], replicated, may hold values from -2 to 2
- relax: float32 [2, 512], replicated, may hold values from 0.3 to 1
Outputs:
- potential: float32 [128, 512, 512], P('axial', 'trans')
The draws below stay inside these ranges and needn't reach their ends.
All inputs are finite; a program needn't handle non-finite values.
Results may differ from the reference program's by a relative error of at most 0.00008.
Values sent between devices are 32-bit elements; how exact they have to be, the bound alone decides.
No kernel may reach another device: no remote copies, remote signals or barrier semaphores. Data moves between devices by JAX's collectives and lax.ppermute only.
A program may use at most 128 MiB of HBM per device.

```python
import math
import jax
import jax.numpy as jnp
from jax import lax

NX = 512
NY = 512
NV = 4
NZ = 128
HALF = 64


def place_ends(entries, rng, low, largest):
    shape = entries.shape
    place = [jax.random.randint(jax.random.fold_in(rng, axis), (), 0, shape[axis]) for axis in range(len(shape))]
    entries = entries.at[tuple(place)].set(low)
    longest = shape.index(max(shape))
    place[longest] = (place[longest] + 1) % shape[longest]
    return entries.at[tuple(place)].set(largest)


def shard_levels(own_key, extent, shards, smallest, top_value):
    loudness = 1.0
    for dim, parts in shards:
        heights = jax.random.uniform(jax.random.fold_in(jax.random.fold_in(own_key, 6), dim), (parts,), jnp.float32, smallest / len(shards), top_value / len(shards))
        loudness = loudness * jnp.repeat(jnp.exp(heights), extent[dim] // parts).reshape((-1,) + (1,) * (len(extent) - 1 - dim))
    return loudness


def centred(own_key, extent, width, most, shards=(), kind=jnp.bfloat16):
    entries = jax.random.normal(own_key, extent, jnp.float32) * width
    if len(shards) > 0:
        entries = shard_levels(own_key, extent, shards, -0.22, 0.18) * entries
    return jnp.clip(entries, min=-most, max=most).astype(kind)


def setup_inputs(seed: int = 0) -> dict:
    arg_keys = jax.random.split(jax.random.key(seed), 5)
    return {
        "source": centred(arg_keys[0], (NZ, NX, NY), 1.0, 6.0, ((0, 16), (1, 2)), jnp.float32),
        "labels": place_ends(jax.random.randint(arg_keys[1], (NZ, NX, NY), 0, NV), jax.random.fold_in(arg_keys[1], 1), 0, NV - 1).astype(jnp.int32),
        "voltages": jnp.clip(jax.random.uniform(arg_keys[2], (NV,), jnp.float32, -2.0, 2.0), -2.0, 2.0),
        "relax": jnp.clip(jnp.exp(jax.random.uniform(arg_keys[3], (2, NX), jnp.float32, math.log(0.3), math.log(1.0))), 0.3, 1.0),
    }


def sine_table(count):
    index = jnp.arange(count, dtype=jnp.float32)
    scale = jnp.sqrt(2.0 / (count + 1.0))
    basis = scale * jnp.sin(jnp.pi * (index[:, None] + 1.0) * (index[None, :] + 1.0) / (count + 1.0))
    eigen = 2.0 - 2.0 * jnp.cos(jnp.pi * (index + 1.0) / (count + 1.0))
    return (basis, eigen)

def reference(source, labels, voltages, relax):
    high = lax.Precision.HIGHEST
    basis_x, eigen_x = sine_table(NX)
    basis_y, eigen_y = sine_table(NY)
    charge = source + voltages[labels]
    flipped = charge[::-1]
    folded = jnp.concatenate([0.5 * (charge[:HALF] + flipped[:HALF]), 0.5 * (charge[HALF:] - flipped[HALF:])], 0)
    inner = jnp.matmul(folded, basis_y.T, precision=high)
    modes = jnp.matmul(basis_x, inner, precision=high)
    diag = eigen_x[:, None] + eigen_y[None, :] + 2.0
    weight = jnp.concatenate([jnp.broadcast_to(relax[0][None, :, None], (HALF, NX, 1)), jnp.broadcast_to(relax[1][None, :, None], (NZ - HALF, NX, 1))], 0)
    first = weight * modes / diag
    zero_plane = jnp.zeros((1, NX, NY), jnp.float32)
    below = jnp.concatenate([zero_plane, first[:-1]], 0)
    above = jnp.concatenate([first[1:], zero_plane], 0)
    second = first + weight * (modes - diag * first + below + above) / diag
    back = jnp.matmul(second, basis_y, precision=high)
    field = jnp.matmul(basis_x.T, back, precision=high)
    signs = jnp.concatenate([-jnp.ones((HALF,), jnp.float32), jnp.ones((NZ - HALF,), jnp.float32)])
    return field + signs[:, None, None] * field[::-1]
```

```python
import jax
import jax.numpy as jnp
import ml_dtypes
import numpy as np
from jax import lax
from jax.experimental import pallas as pl
from jax.experimental.pallas import tpu as pltpu
from jax.sharding import PartitionSpec as P

NX = 512
NY = 512
F32 = jnp.float32
BF16 = jnp.bfloat16
VMEM_LIMIT = 48 * 1024 * 1024


def table_parts():
    f = np.float32
    index = np.arange(NX, dtype=f) + f(1)
    inverse = f(1) / f(NX + 1)
    angle = ((f(np.pi) * index[:, None]) * index[None, :]) * inverse
    basis = np.sqrt(f(2) / f(NX + 1)).astype(f) * np.sin(angle.astype(np.float64)).astype(f)
    high = basis.astype(ml_dtypes.bfloat16)
    low = (basis - high.astype(f)).astype(ml_dtypes.bfloat16)
    return high, low


BASIS = table_parts()
BASIS_T = tuple(np.ascontiguousarray(part.T) for part in BASIS)


def split(x):
    high = x.astype(BF16)
    return high, (x - high.astype(F32)).astype(BF16)


def dot3(left, right):
    def dot(a, b):
        return jnp.dot(a, b, preferred_element_type=F32)

    return dot(left[0], right[0]) + (dot(left[0], right[1]) + dot(left[1], right[0]))


def after(value, *others):
    return lax.optimization_barrier((value,) + others)[0]


def whole(shape):
    return pl.BlockSpec(shape, lambda g: (0,) * len(shape))


def call(body, grid, in_specs, out_specs, out_shape, flops, size, scratch=(), aliases=None):
    return pl.pallas_call(
        body,
        grid=(grid,),
        in_specs=in_specs,
        out_specs=out_specs,
        out_shape=out_shape,
        scratch_shapes=scratch,
        input_output_aliases=aliases or {},
        compiler_params=pltpu.CompilerParams(
            dimension_semantics=("arbitrary",), vmem_limit_bytes=VMEM_LIMIT
        ),
        cost_estimate=pl.CostEstimate(flops=flops, bytes_accessed=size, transcendentals=0),
    )


def rows_body(volts, source, labels, high, low, out):
    label = labels[...]
    pick = jnp.full(label.shape, volts[0], F32)
    for region in range(1, volts.shape[0]):
        pick = jnp.where(label == region, volts[region], pick)
    out[...] = dot3(split(source[...] + pick), (high[...], low[...]))


def row_modes(source, labels, voltages, chunk):
    rows = source.shape[1]
    count, start, step = chunk
    plane = pl.BlockSpec((None, rows, NY), lambda g: (start + step * g, 0, 0))
    return call(
        rows_body,
        count,
        [pl.BlockSpec(memory_space=pltpu.SMEM), plane, plane, whole((NY, NY)), whole((NY, NY))],
        pl.BlockSpec((None, rows, NY), lambda g: (g, 0, 0)),
        jax.ShapeDtypeStruct((count, rows, NY), F32),
        6 * count * rows * NY * NY,
        12 * count * rows * NY,
    )(voltages, source, labels, jnp.asarray(BASIS_T[0]), jnp.asarray(BASIS_T[1]))


def modes_body(parts, aliased):
    def body(*refs):
        high, low = refs[:2]
        rows = [ref[...] for ref in refs[2:2 + parts]]
        out = refs[2 + parts + aliased]
        out[...] = dot3((high[...], low[...]), split(jnp.concatenate(rows, axis=0)))

    return body


def x_modes(table, parts, total, chunk, buffer):
    rows = parts[0].shape[1]
    count, start, step = chunk
    plane = pl.BlockSpec((None, rows, NY), lambda g: (g, 0, 0))
    aliased = 0 if buffer is None else 1
    return call(
        modes_body(len(parts), aliased),
        count,
        [whole((NX, NX))] * 2 + [plane] * len(parts) + [pl.BlockSpec(memory_space=pl.ANY)] * aliased,
        pl.BlockSpec((None, NX, NY), lambda g: (start + step * g, 0, 0)),
        jax.ShapeDtypeStruct((total, NX, NY), F32),
        6 * count * NX * NX * NY,
        8 * count * NX * NY,
        aliases={2 + len(parts): 0} if aliased else None,
    )(*table, *parts, *([buffer] if aliased else []))


def stencil(inverse, weights, own, other, last_plane, plane, extra):
    keep_low = jnp.where(plane > 0, 1.0, 0.0)
    keep_high = jnp.where(plane < last_plane, 1.0, 0.0)
    edge = 1.0 - keep_low * keep_high
    inv = inverse[...]
    near = weights[:, 0:1] * own[1][...] + weights[:, 1:2] * other[1][...]
    far = weights[:, 2:3] * (keep_low * own[0][...] + keep_high * own[2][...])
    far = far + weights[:, 3:4] * (keep_low * other[0][...] + keep_high * other[2][...])
    return inv * (near + inv * far) + edge * extra[...]


def back_to_grid(total, rows_table, table):
    return dot3(split(dot3(rows_table, split(total))), table)


def halves(refs):
    return tuple(ref[...] for ref in refs)


def plane_specs(place, last_plane):
    def at(shift):
        def index(g):
            return (jnp.clip(place(g) + shift, 0, last_plane), 0, 0)

        return pl.BlockSpec((None, NX, NY), index)

    return [at(-1), at(0), at(1)]


def extra_spec(place, middle):
    return pl.BlockSpec((None, NX, NY), lambda g: (jnp.where(place(g) < middle, 0, 1), 0, 0))


def finished_planes(count, place, inverse, weights, own, other, extra, rows_table, table, buffer):
    total, rows = own.shape[0], rows_table[0].shape[0]
    aliased = 0 if buffer is None else 1

    def body(*refs):
        inv, wts = refs[:2]
        out = refs[-1]
        modes = stencil(inv, wts, refs[2:5], refs[5:8], total - 1, place(pl.program_id(0)), refs[8])
        out[...] = back_to_grid(modes, halves(refs[9:11]), halves(refs[11:13]))

    return call(
        body,
        count,
        [whole((NX, NY)), whole((NX, 128))]
        + plane_specs(place, total - 1) * 2
        + [extra_spec(place, total // 2)]
        + [whole((rows, NX))] * 2 + [whole((NY, NY))] * 2
        + [pl.BlockSpec(memory_space=pl.ANY)] * aliased,
        pl.BlockSpec((None, rows, NY), lambda g: (place(g), 0, 0)),
        jax.ShapeDtypeStruct((total, rows, NY), F32),
        count * (6 * rows * NX * NY + 6 * rows * NY * NY),
        count * 28 * NX * NY,
        aliases={13: 0} if aliased else None,
    )(inverse, weights, *[own] * 3, *[other] * 3, extra, *rows_table, *table, *([buffer] if aliased else []))


def base_planes(start, missing, inverse, weights, own, other, extra):
    total = own.shape[0]

    def place(g):
        return start + g

    def body(*refs):
        plane = place(pl.program_id(0))
        others = [jnp.where(plane + shift == missing, 0.0, ref[...]) for shift, ref in zip((-1, 0, 1), refs[5:8])]
        refs[-1][...] = stencil(refs[0], refs[1], refs[2:5], others, total - 1, plane, refs[8])

    return call(
        body,
        3,
        [whole((NX, NY)), whole((NX, 128))] + plane_specs(place, total - 1) * 2 + [extra_spec(place, total // 2)],
        pl.BlockSpec((None, NX, NY), lambda g: (g, 0, 0)),
        jax.ShapeDtypeStruct((3, NX, NY), F32),
        3 * 12 * NX * NY,
        3 * 32 * NX * NY,
    )(inverse, weights, *[own] * 3, *[other] * 3, extra)


def last_planes(start, inverse, weights, base, x_table, parts, rows_table, table, buffer):
    total, rows = buffer.shape[0], buffer.shape[1]
    count = len(parts)

    def body(*refs):
        inv, wts, base_ref = refs[:3]
        pieces = refs[5:5 + count]
        near_rows, grid_table = refs[5 + count:7 + count], refs[7 + count:9 + count]
        out, late = refs[-2:]
        step = pl.program_id(0)

        @pl.when(step == 0)
        def _():
            rows_in = jnp.concatenate([ref[...] for ref in pieces], axis=0)
            late[...] = dot3(halves(refs[3:5]), split(rows_in))

        scale = jnp.where(step == 1, 1.0, 0.0)
        factor = scale * wts[:, 1:2] + (1.0 - scale) * inv[...] * wts[:, 3:4]
        modes = base_ref[...] + inv[...] * (factor * late[...])
        out[...] = back_to_grid(modes, halves(near_rows), halves(grid_table))

    length = parts[0].shape[1]
    width = x_table[0].shape[1]
    return call(
        body,
        3,
        [whole((NX, NY)), whole((NX, 128)), pl.BlockSpec((None, NX, NY), lambda g: (g, 0, 0))]
        + [whole((NX, width))] * 2
        + [pl.BlockSpec((None, length, NY), lambda g: (0, 0, 0))] * count
        + [whole((rows, NX))] * 2 + [whole((NY, NY))] * 2 + [pl.BlockSpec(memory_space=pl.ANY)],
        pl.BlockSpec((None, rows, NY), lambda g: (start + g, 0, 0)),
        jax.ShapeDtypeStruct((total, rows, NY), F32),
        6 * NX * width * NY + 3 * (6 * rows * NX * NY + 6 * rows * NY * NY),
        3 * 8 * NX * NY,
        scratch=[pltpu.VMEM((NX, NY), F32)],
        aliases={9 + count: 0},
    )(inverse, weights, base, *x_table, *parts, *rows_table, *table, buffer)


def to_mirror(block):
    count = lax.axis_size("axial")
    return lax.ppermute(block, "axial", [(i, count - 1 - i) for i in range(count)])


def gather_rows(block):
    count = lax.axis_size("trans")
    parts = [block]
    for step in range(1, count):
        route = [(i, (i - step) % count) for i in range(count)]
        parts.append(lax.ppermute(block, "trans", route))
    return parts


def halo(first, last):
    count = lax.axis_size("axial")
    up = [(i, i + 1) for i in range(count - 1) if i + 1 != count // 2]
    below = lax.ppermute(last, "axial", up)
    above = lax.ppermute(first, "axial", [(j, i) for i, j in up])
    return below, above


def on_device(source, labels, voltages, relax):
    planes, rows = source.shape[0], source.shape[1]
    half = planes // 2
    ax_count = lax.axis_size("axial")
    position = lax.axis_index("axial")
    row_start = lax.axis_index("trans") * rows

    chunk_a = (2, 0, planes - 1)
    chunk_b = (half - 2, 1, 1)
    chunk_c = (half - 2, half + 1, 1)
    chunk_d = (1, half - 1, 1)
    chunk_e = (1, half, 1)
    chunks = [chunk_a, chunk_b, chunk_c, chunk_d, chunk_e]

    def mirrored(chunk):
        return chunk[0], planes - 1 - chunk[1], -chunk[2]

    inner = [row_modes(source, labels, voltages, chunk) for chunk in chunks]

    x_table = tuple(
        lax.dynamic_slice_in_dim(jnp.concatenate([part, part], axis=1), row_start, NX, 1)
        for part in (jnp.asarray(BASIS[0]), jnp.asarray(BASIS[1]))
    )
    rows_table = tuple(
        lax.dynamic_slice_in_dim(jnp.asarray(part), row_start, rows, 0) for part in BASIS_T
    )
    table = tuple(jnp.asarray(part) for part in BASIS)

    index = jnp.arange(NX, dtype=F32) + 1.0
    eigen = 2.0 - 2.0 * jnp.cos(jnp.pi * index / (NX + 1.0))
    inverse = 1.0 / (eigen[:, None] + eigen[None, :] + 2.0)
    even, odd = relax[0], relax[1]
    a_even, a_odd = (2.0 - even) * even, (2.0 - odd) * odd
    b_even, b_odd = even * even, odd * odd
    columns = [0.5 * (a_even + a_odd), 0.5 * (a_even - a_odd), 0.5 * (b_even + b_odd), 0.5 * (b_even - b_odd)]
    weights = jnp.pad(jnp.stack(columns, axis=1), ((0, 0), (0, 124)))
    beta, beta_cross = columns[2][:, None], columns[3][:, None]
    cross = (even * odd)[:, None] * inverse * inverse

    m_a, o_a = to_mirror(inner[0]), gather_rows(inner[0])
    m_b, o_b = to_mirror(inner[1]), gather_rows(inner[1])
    own = x_modes(x_table, o_a, planes, chunk_a, None)
    below, above = halo(own[0], own[planes - 1])
    m_c = to_mirror(after(inner[2], m_a))
    x_a = gather_rows(m_a)
    o_c = gather_rows(after(inner[2], own))
    own = x_modes(x_table, o_b, planes, chunk_b, own)
    other = x_modes(x_table, x_a, planes, mirrored(chunk_a), None)
    below_2, above_2 = halo(other[0], other[planes - 1])
    m_d = to_mirror(after(inner[3], m_b))
    x_b = gather_rows(m_b)
    o_d = gather_rows(after(inner[3], own))
    own = x_modes(x_table, o_c, planes, chunk_c, own)
    o_e = gather_rows(after(inner[4], own))
    other = x_modes(x_table, x_b, planes, mirrored(chunk_b), other)
    own = x_modes(x_table, o_d, planes, chunk_d, own)
    m_e = to_mirror(after(inner[4], m_c))
    x_c = gather_rows(m_c)
    own = x_modes(x_table, o_e, planes, chunk_e, own)
    at_bottom = jnp.where(position == ax_count // 2, 1.0, 0.0)
    at_top = jnp.where(position == ax_count // 2 - 1, 1.0, 0.0)
    extra = jnp.stack([
        inverse * inverse * (beta * below + beta_cross * below_2) + at_bottom * cross * own[0],
        inverse * inverse * (beta * above + beta_cross * above_2) - at_top * cross * own[planes - 1],
    ])
    other = x_modes(x_table, x_c, planes, mirrored(chunk_c), other)

    def outer(g):
        return jnp.where(g < half - 2, g, g + 4)

    out = finished_planes(
        planes - 4, outer, inverse, weights, own, other, extra, rows_table, table, None
    )
    x_d = gather_rows(m_d)
    other = x_modes(x_table, x_d, planes, mirrored(chunk_d), other)
    base = base_planes(half - 2, half - 1, inverse, weights, own, other, extra)
    out = finished_planes(
        1, lambda g: g + half + 1, inverse, weights, own, other, extra, rows_table, table, out
    )
    x_e = gather_rows(m_e)
    return last_planes(half - 2, inverse, weights, base, x_table, x_e, rows_table, table, out)


def solution(mesh):
    placed = (P("axial", "trans", None), P("axial", "trans", None), P(), P())
    return jax.shard_map(
        on_device, mesh=mesh, in_specs=placed, out_specs=P("axial", "trans", None), check_vma=False
    )
```

```python
import functools

import jax
import jax.numpy as jnp
import ml_dtypes
import numpy as np
from jax import lax
from jax.experimental import pallas as pl
from jax.experimental.pallas import tpu as pltpu
from jax.sharding import PartitionSpec as P

NX = 512
NY = 512
F32 = jnp.float32
BF16 = jnp.bfloat16
VMEM_LIMIT = 60 * 1024 * 1024


def table_parts():
    f = np.float32
    index = np.arange(NX, dtype=f) + f(1)
    inverse = f(1) / f(NX + 1)
    angle = ((f(np.pi) * index[:, None]) * index[None, :]) * inverse
    basis = np.sqrt(f(2) / f(NX + 1)).astype(f) * np.sin(angle.astype(np.float64)).astype(f)
    high = basis.astype(ml_dtypes.bfloat16)
    low = (basis - high.astype(f)).astype(ml_dtypes.bfloat16)
    return high, low


BASIS = table_parts()
BASIS_T = tuple(np.ascontiguousarray(part.T) for part in BASIS)


def split(x):
    high = x.astype(BF16)
    return high, (x - high.astype(F32)).astype(BF16)


def dot3(left, right):
    def dot(a, b):
        return jnp.dot(a, b, preferred_element_type=F32)

    return dot(left[0], right[0]) + (dot(left[0], right[1]) + dot(left[1], right[0]))


def after(value, *others):
    return lax.optimization_barrier((value,) + others)[0]


def whole(shape):
    return pl.BlockSpec(shape, lambda g: (0,) * len(shape))


def call(body, grid, in_specs, out_specs, out_shape, cost, scratch=(), aliases=None):
    return pl.pallas_call(
        body,
        grid=(grid,),
        in_specs=in_specs,
        out_specs=out_specs,
        out_shape=out_shape,
        scratch_shapes=scratch,
        input_output_aliases=aliases or {},
        compiler_params=pltpu.CompilerParams(
            dimension_semantics=("arbitrary",), vmem_limit_bytes=VMEM_LIMIT
        ),
        cost_estimate=pl.CostEstimate(flops=cost[0], bytes_accessed=cost[1], transcendentals=0),
    )


COST = {
    "rows": (1, 1),
    "modes": (1, 1),
    "own": (1, 1),
    "first": (1, 1),
    "next": (1, 1),
    "step": (1, 1),
    "base": (1, 1),
    "last": (1, 1),
}


def halves(refs):
    return tuple(ref[...] for ref in refs)


def joined(refs):
    return split(jnp.concatenate([ref[...] for ref in refs], axis=0))


def row_modes(source, labels, voltages, planes, uses):
    rows = source.shape[1]
    first, stride = planes[0], planes[1] - planes[0]
    count = len(planes)

    def body(volts, source_ref, labels_ref, high, low, *outs):
        label = labels_ref[...]
        pick = jnp.full(label.shape, volts[0], F32)
        for region in range(1, volts.shape[0]):
            pick = jnp.where(label == region, volts[region], pick)
        modes = dot3(split(source_ref[...] + pick), (high[...], low[...]))
        g = pl.program_id(0)
        for use, out in zip(uses, outs):
            start = planes.index(use[0])
            if len(use) == count:
                out[...] = modes
            else:
                pl.when((g >= start) & (g < start + len(use)))(functools.partial(put, out, modes))

    block = pl.BlockSpec((None, rows, NY), lambda g: (first + stride * g, 0, 0))

    def slot(use):
        start, last = planes.index(use[0]), len(use) - 1
        return pl.BlockSpec((None, rows, NY), lambda g: (jnp.clip(g - start, 0, last), 0, 0))

    return call(
        body,
        count,
        [pl.BlockSpec(memory_space=pltpu.SMEM), block, block, whole((NY, NY)), whole((NY, NY))],
        [slot(use) for use in uses],
        [jax.ShapeDtypeStruct((len(use), rows, NY), F32) for use in uses],
        COST["rows"],
    )(voltages, source, labels, *[jnp.asarray(part) for part in BASIS_T])


def put(out, value):
    out[...] = value


def own_part(flags, inverse, weights, table, ends, others):
    count = len(ends)
    rows = ends[0].shape[1]
    total = 2 + others[0].shape[0]

    def stack(slots, slot):
        return [pl.BlockSpec((None, rows, NY), lambda g: (jnp.clip(slot(g), 0, slots - 1), 0, 0))] * count

    def body(flag, inv_ref, wts, *refs):
        th, tl = refs[:2]
        end_refs, other_refs = refs[2:2 + count], refs[2 + count:2 + 2 * count]
        out, first_out, last_out, ring = refs[2 + 2 * count:]
        g = pl.program_id(0)

        def load(group):
            ring[lax.rem(g, 3)] = dot3(halves((th, tl)), joined(group))

        pl.when((g == 0) | (g == total - 1))(lambda: load(end_refs))
        pl.when((g > 0) & (g < total - 1))(lambda: load(other_refs))

        @pl.when(g == 0)
        def _():
            first_out[...] = ring[0]

        @pl.when(g == total - 1)
        def _():
            last_out[...] = ring[(total - 1) % 3]

        @pl.when(g > 0)
        def _():
            plane = g - 1
            bottom, top = plane == 0, plane == total - 1
            mid, inv = ring[lax.rem(plane, 3)], inv_ref[...]
            below = jnp.where(bottom, 0.0, ring[lax.rem(plane + 2, 3)])
            above = jnp.where(top, 0.0, ring[lax.rem(plane + 1, 3)])
            turn = jnp.where(bottom, flag[0], 0.0) - jnp.where(top, flag[1], 0.0)
            far = wts[:, 2:3] * (below + above) + (turn * wts[:, 4:5]) * mid
            out[...] = inv * (wts[:, 0:1] * mid + inv * far)

    return call(
        body,
        total + 1,
        [pl.BlockSpec(memory_space=pltpu.SMEM), whole((NX, NY)), whole((NX, 128))]
        + [whole((NX, NX))] * 2
        + stack(2, lambda g: jnp.where(g > 0, 1, 0))
        + stack(total - 2, lambda g: total - 2 - g),
        [
            pl.BlockSpec((None, NX, NY), lambda g: (jnp.maximum(g - 1, 0), 0, 0)),
            whole((NX, NY)),
            whole((NX, NY)),
        ],
        [
            jax.ShapeDtypeStruct((total, NX, NY), F32),
            jax.ShapeDtypeStruct((NX, NY), F32),
            jax.ShapeDtypeStruct((NX, NY), F32),
        ],
        COST["own"],
        scratch=[pltpu.VMEM((3, NX, NY), F32)],
    )(flags, inverse, weights, *table, *ends, *others)


def part_specs(parts, slot):
    return [pl.BlockSpec((None,) + part.shape[1:], lambda g: (slot, 0, 0)) for part in parts]


def first_planes(inverse, weights, x_table, outer, inner, partial, own_first, own_last, rows_table, table):
    count, total, rows = len(outer), partial.shape[0], rows_table[0].shape[0]

    def body(*refs):
        inv, wts = refs[:2]
        outer_refs, inner_refs = refs[4:4 + count], refs[4 + count:4 + 2 * count]
        part, first_ref, last_ref = refs[4 + 2 * count:7 + 2 * count]
        near_rows, grid_table = refs[7 + 2 * count:9 + 2 * count], refs[9 + 2 * count:11 + 2 * count]
        top, plane_0, plane_1, plane_2, to_above, to_below, out = refs[-7:]
        g = pl.program_id(0)

        def fill(target, group):
            target[...] = dot3(halves(refs[2:4]), joined(group))

        @pl.when(g == 0)
        def _():
            fill(top, outer_refs)
            to_above[...] = wts[:, 2:3] * last_ref[...] + wts[:, 3:4] * top[...]

        @pl.when(g == 1)
        def _():
            fill(plane_0, outer_refs)
            to_below[...] = wts[:, 2:3] * first_ref[...] + wts[:, 3:4] * plane_0[...]

        @pl.when(g == 2)
        def _():
            fill(plane_1, inner_refs)

        @pl.when(g == 3)
        def _():
            fill(plane_2, inner_refs)
            modes = part[...] + other_part(inv[...], wts, plane_0[...], plane_1[...], plane_2[...])
            out[...] = dot3(split(dot3(halves(near_rows), split(modes))), halves(grid_table))

    stack = (None,) + outer[0].shape[1:]
    return call(
        body,
        4,
        [whole((NX, NY)), whole((NX, 128))] + [whole((NX, NX))] * 2
        + [pl.BlockSpec(stack, lambda g: (jnp.minimum(g, 1), 0, 0))] * count
        + [pl.BlockSpec(stack, lambda g: (jnp.maximum(g - 2, 0), 0, 0))] * count
        + [pl.BlockSpec((None, NX, NY), lambda g: (1, 0, 0))] + [whole((NX, NY))] * 2
        + [whole((rows, NX))] * 2 + [whole((NY, NY))] * 2,
        [whole((NX, NY))] * 6 + [pl.BlockSpec((None, rows, NY), lambda g: (1, 0, 0))],
        [jax.ShapeDtypeStruct((NX, NY), F32)] * 6 + [jax.ShapeDtypeStruct((total, rows, NY), F32)],
        COST["first"],
    )(inverse, weights, *x_table, *outer, *inner, partial, own_first, own_last, *rows_table, *table)


def next_planes(inverse, weights, x_table, parts, partial, place, low, mid, rows_table, table, buffer):
    count, total, rows = len(parts), partial.shape[0], rows_table[0].shape[0]

    def body(*refs):
        inv, wts = refs[:2]
        part, low_ref, mid_ref = refs[4 + count:7 + count]
        near_rows, grid_table = refs[7 + count:9 + count], refs[9 + count:11 + count]
        high_out, higher_out, out = refs[-3:]
        g = pl.program_id(0)

        def finish(target, *planes):
            target[...] = dot3(halves(refs[2:4]), joined(refs[4:4 + count]))
            modes = part[...] + other_part(inv[...], wts, *[plane[...] for plane in planes], target[...])
            out[...] = dot3(split(dot3(halves(near_rows), split(modes))), halves(grid_table))

        pl.when(g == 0)(lambda: finish(high_out, low_ref, mid_ref))
        pl.when(g == 1)(lambda: finish(higher_out, mid_ref, high_out))

    return call(
        body,
        2,
        [whole((NX, NY)), whole((NX, 128))] + [whole((NX, NX))] * 2
        + [pl.BlockSpec((None,) + parts[0].shape[1:], lambda g: (g, 0, 0))] * count
        + [pl.BlockSpec((None, NX, NY), lambda g: (place + g, 0, 0))] + [whole((NX, NY))] * 2
        + [whole((rows, NX))] * 2 + [whole((NY, NY))] * 2 + [pl.BlockSpec(memory_space=pl.ANY)],
        [whole((NX, NY))] * 2 + [pl.BlockSpec((None, rows, NY), lambda g: (place + g, 0, 0))],
        [jax.ShapeDtypeStruct((NX, NY), F32)] * 2 + [jax.ShapeDtypeStruct((total, rows, NY), F32)],
        COST["next"],
        aliases={11 + count: 2},
    )(inverse, weights, *x_table, *parts, partial, low, mid, *rows_table, *table, buffer)


def end_plane(inverse, weights, partial, mid, high, edge, rows_table, table, buffer):
    rows = rows_table[0].shape[0]

    def body(inv_ref, wts, part, mid_ref, high_ref, edge_ref, *refs):
        inv = inv_ref[...]
        modes = part[...] + other_part(inv, wts, None, mid_ref[...], high_ref[...]) + inv * inv * edge_ref[...]
        refs[-1][...] = dot3(split(dot3(halves(refs[:2]), split(modes))), halves(refs[2:4]))

    return call(
        body,
        1,
        [whole((NX, NY)), whole((NX, 128)), pl.BlockSpec((None, NX, NY), lambda g: (0, 0, 0))]
        + [whole((NX, NY))] * 3 + [whole((rows, NX))] * 2 + [whole((NY, NY))] * 2
        + [pl.BlockSpec(memory_space=pl.ANY)],
        pl.BlockSpec((None, rows, NY), lambda g: (0, 0, 0)),
        jax.ShapeDtypeStruct(buffer.shape, F32),
        COST["step"],
        aliases={10: 0},
    )(inverse, weights, partial, mid, high, edge, *rows_table, *table, buffer)


def other_part(inv, wts, low, mid, high):
    far = low if high is None else high if low is None else low + high
    return inv * (wts[:, 1:2] * mid + inv * (wts[:, 3:4] * far))


def step(inverse, weights, x_table, parts, slot, partial, place, low, mid, rows_table, table, buffer):
    total, rows, count = partial.shape[0], rows_table[0].shape[0], len(parts)
    aliased = 0 if buffer is None else 1

    def body(*refs):
        inv, wts = refs[:2]
        part, low_ref, mid_ref = refs[4 + count:7 + count]
        near_rows, grid_table = refs[7 + count:9 + count], refs[9 + count:11 + count]
        high_out, out = refs[-2:]
        high = dot3(halves(refs[2:4]), joined(refs[4:4 + count]))
        high_out[...] = high
        modes = part[...] + other_part(inv[...], wts, low_ref[...], mid_ref[...], high)
        out[...] = dot3(split(dot3(halves(near_rows), split(modes))), halves(grid_table))

    return call(
        body,
        1,
        [whole((NX, NY)), whole((NX, 128))] + [whole((NX, NX))] * 2 + part_specs(parts, slot)
        + [pl.BlockSpec((None, NX, NY), lambda g: (place, 0, 0))] + [whole((NX, NY))] * 2
        + [whole((rows, NX))] * 2 + [whole((NY, NY))] * 2 + [pl.BlockSpec(memory_space=pl.ANY)] * aliased,
        [whole((NX, NY)), pl.BlockSpec((None, rows, NY), lambda g: (place, 0, 0))],
        [jax.ShapeDtypeStruct((NX, NY), F32), jax.ShapeDtypeStruct((total, rows, NY), F32)],
        COST["step"],
        aliases={11 + count: 1} if aliased else None,
    )(inverse, weights, *x_table, *parts, partial, low, mid, *rows_table, *table, *([buffer] if aliased else []))


def last_planes(inverse, weights, partial, x_table, parts, before, early, top, edge, rows_table, table, buffer):
    total, rows = buffer.shape[0], buffer.shape[1]
    count = len(parts)

    def body(*refs):
        inv_ref, wts, part = refs[:3]
        before_ref, early_ref, top_ref, edge_ref = refs[5 + count:9 + count]
        near_rows, grid_table = refs[9 + count:11 + count], refs[11 + count:13 + count]
        out, late = refs[-2:]
        g = pl.program_id(0)

        def finish(low, mid, high, edge=None):
            inv = inv_ref[...]
            far = wts[:, 3:4] * (low[...] if high is None else low[...] + high[...])
            if edge is not None:
                far = far + edge[...]
            modes = part[...] + inv * (wts[:, 1:2] * mid[...] + inv * far)
            out[...] = dot3(split(dot3(halves(near_rows), split(modes))), halves(grid_table))

        @pl.when(g == 0)
        def _():
            late[...] = dot3(halves(refs[3:5]), joined(refs[5:5 + count]))
            finish(before_ref, early_ref, late)

        pl.when(g == 1)(lambda: finish(early_ref, late, top_ref))
        pl.when(g == 2)(lambda: finish(late, top_ref, None, edge_ref))

    return call(
        body,
        3,
        [whole((NX, NY)), whole((NX, 128)), pl.BlockSpec((None, NX, NY), lambda g: (total - 3 + g, 0, 0))]
        + [whole((NX, NX))] * 2 + part_specs(parts, 0) + [whole((NX, NY))] * 4
        + [whole((rows, NX))] * 2 + [whole((NY, NY))] * 2 + [pl.BlockSpec(memory_space=pl.ANY)],
        pl.BlockSpec((None, rows, NY), lambda g: (total - 3 + g, 0, 0)),
        jax.ShapeDtypeStruct((total, rows, NY), F32),
        COST["last"],
        scratch=[pltpu.VMEM((NX, NY), F32)],
        aliases={13 + count: 0},
    )(inverse, weights, partial, *x_table, *parts, before, early, top, edge, *rows_table, *table, buffer)


def to_mirror(block):
    count = lax.axis_size("axial")
    return lax.ppermute(block, "axial", [(i, count - 1 - i) for i in range(count)])


def gather_rows(block):
    count = lax.axis_size("trans")
    parts = [block]
    for step in range(1, count):
        route = [(i, (i - step) % count) for i in range(count)]
        parts.append(lax.ppermute(block, "trans", route))
    return parts


def halo(first, last):
    count = lax.axis_size("axial")
    up = [(i, i + 1) for i in range(count - 1) if i + 1 != count // 2]
    below = lax.ppermute(last, "axial", up)
    above = lax.ppermute(first, "axial", [(j, i) for i, j in up])
    return below, above


def on_device(source, labels, voltages, relax):
    planes, rows = source.shape[0], source.shape[1]
    half, end = planes // 2, planes - 1
    ax_count = lax.axis_size("axial")
    position = lax.axis_index("axial")
    row_start = lax.axis_index("trans") * rows

    inner = list(range(end - 1, 0, -1))
    chunks = [[0, end], inner[:2], inner[2:4]] + [[plane] for plane in inner[4:]]
    (ends,) = row_modes(source, labels, voltages, [0, end], [[0, end]])
    others, *rest = row_modes(source, labels, after(voltages, ends), inner, [inner] + chunks[1:])
    ends, others = gather_rows(ends), gather_rows(others)
    sent = []
    for number, block in enumerate([ends[0]] + rest):
        if number < 3:
            sent.append(to_mirror(block))

    x_table = tuple(
        lax.dynamic_slice_in_dim(jnp.concatenate([part, part], axis=1), row_start, NX, 1)
        for part in (jnp.asarray(BASIS[0]), jnp.asarray(BASIS[1]))
    )
    rows_table = tuple(
        lax.dynamic_slice_in_dim(jnp.asarray(part), row_start, rows, 0) for part in BASIS_T
    )
    table = tuple(jnp.asarray(part) for part in BASIS)

    index = jnp.arange(NX, dtype=F32) + 1.0
    eigen = 2.0 - 2.0 * jnp.cos(jnp.pi * index / (NX + 1.0))
    inverse = 1.0 / (eigen[:, None] + eigen[None, :] + 2.0)
    even, odd = relax[0], relax[1]
    a_even, a_odd = (2.0 - even) * even, (2.0 - odd) * odd
    b_even, b_odd = even * even, odd * odd
    columns = [
        0.5 * (a_even + a_odd),
        0.5 * (a_even - a_odd),
        0.5 * (b_even + b_odd),
        0.5 * (b_even - b_odd),
        even * odd,
    ]
    weights = jnp.pad(jnp.stack(columns, axis=1), ((0, 0), (0, 128 - len(columns))))
    flags = jnp.stack([position == ax_count // 2, position == ax_count // 2 - 1]).astype(F32)

    passed = [gather_rows(after(sent[0], *x_table, *rows_table, inverse, weights, flags))]
    partial, own_first, own_last = own_part(flags, inverse, weights, x_table, ends, others)
    passed.append(gather_rows(sent[1]))
    sent += [to_mirror(after(block, passed[1][-1], partial)) for block in rest[2:]]
    passed.append(gather_rows(after(sent[2], partial)))
    top, plane_0, low, mid, to_above, to_below, out = first_planes(
        inverse, weights, x_table, [after(passed[0][0], sent[2])] + passed[0][1:], passed[1],
        partial, own_first, own_last, rows_table, table,
    )
    plane_1 = low
    passed.append(gather_rows(after(sent[-2], out)))
    for number in range(2, len(sent) - 2):
        low, mid, out = next_planes(
            inverse, weights, x_table, passed[number], partial, 2 * number - 2, low, mid, rows_table, table, out
        )
    below, above = halo(after(to_below, sent[-1]), after(to_above, sent[-1]))
    final = gather_rows(sent[-1])
    high, out = step(
        inverse, weights, x_table, [after(passed[-1][0], sent[-1])] + passed[-1][1:], 0,
        partial, planes - 4, low, mid, rows_table, table, out,
    )
    low, mid = mid, high
    out = end_plane(inverse, weights, partial, plane_0, plane_1, below, rows_table, table, out)
    return last_planes(
        inverse, weights, partial, x_table, final, low, mid, top, above, rows_table, table, out
    )


def solution(mesh):
    placed = (P("axial", "trans", None), P("axial", "trans", None), P(), P())
    return jax.shard_map(
        on_device, mesh=mesh, in_specs=placed, out_specs=P("axial", "trans", None), check_vma=False
    )
```

```python
import functools

import jax
import jax.numpy as jnp
import ml_dtypes
import numpy as np
from jax import lax
from jax.experimental import pallas as pl
from jax.experimental.pallas import tpu as pltpu
from jax.sharding import PartitionSpec as P

NX = 512
NY = 512
F32 = jnp.float32
BF16 = jnp.bfloat16
VMEM_LIMIT = 60 * 1024 * 1024


def table_parts():
    f = np.float32
    index = np.arange(NX, dtype=f) + f(1)
    inverse = f(1) / f(NX + 1)
    angle = ((f(np.pi) * index[:, None]) * index[None, :]) * inverse
    basis = np.sqrt(f(2) / f(NX + 1)).astype(f) * np.sin(angle.astype(np.float64)).astype(f)
    high = basis.astype(ml_dtypes.bfloat16)
    low = (basis - high.astype(f)).astype(ml_dtypes.bfloat16)
    return high, low


BASIS = table_parts()
BASIS_T = tuple(np.ascontiguousarray(part.T) for part in BASIS)


def split(x):
    high = x.astype(BF16)
    return high, (x - high.astype(F32)).astype(BF16)


def dot3(left, right):
    def dot(a, b):
        return jnp.dot(a, b, preferred_element_type=F32)

    return dot(left[0], right[0]) + (dot(left[0], right[1]) + dot(left[1], right[0]))


def after(value, *others):
    return lax.optimization_barrier((value,) + others)[0]


def whole(shape):
    return pl.BlockSpec(shape, lambda g: (0,) * len(shape))


def call(body, grid, in_specs, out_specs, out_shape, cost, scratch=(), aliases=None):
    return pl.pallas_call(
        body,
        grid=(grid,),
        in_specs=in_specs,
        out_specs=out_specs,
        out_shape=out_shape,
        scratch_shapes=scratch,
        input_output_aliases=aliases or {},
        compiler_params=pltpu.CompilerParams(
            dimension_semantics=("arbitrary",), vmem_limit_bytes=VMEM_LIMIT
        ),
        cost_estimate=pl.CostEstimate(flops=cost[0], bytes_accessed=cost[1], transcendentals=0),
    )


COST = {
    "rows": (1, 1),
    "modes": (1, 1),
    "own": (1, 1),
    "first": (1, 1),
    "next": (1, 1),
    "step": (1, 1),
    "base": (1, 1),
    "last": (1, 1),
}


def halves(refs):
    return tuple(ref[...] for ref in refs)


def joined(refs):
    return split(jnp.concatenate([ref[...] for ref in refs], axis=0))


def row_modes(source, labels, voltages, planes, uses):
    rows = source.shape[1]
    steps = len(planes) // 2

    def body(volts, *refs):
        high, low = refs[4:6]
        charge = []
        for source_ref, labels_ref in (refs[0:2], refs[2:4]):
            label = labels_ref[...]
            pick = jnp.full(label.shape, volts[0], F32)
            for region in range(1, volts.shape[0]):
                pick = jnp.where(label == region, volts[region], pick)
            charge.append(source_ref[...] + pick)
        modes = dot3(split(jnp.concatenate(charge, axis=0)), (high[...], low[...]))
        modes = modes.reshape(2, rows, NY)
        g = pl.program_id(0)
        for use, out in zip(uses, refs[6:]):
            start = planes.index(use[0])
            if len(use) == len(planes):
                out[...] = modes
            else:
                part = modes if len(use) == 2 else modes[start % 2:start % 2 + 1]
                pl.when(g == start // 2)(functools.partial(put, out, part))

    def block(which):
        if steps == 1:
            return pl.BlockSpec((None, rows, NY), lambda g: (planes[which], 0, 0))
        return pl.BlockSpec((None, rows, NY), lambda g: (planes[which] - 2 * g, 0, 0))

    def slot(use):
        if len(use) == len(planes):
            return pl.BlockSpec((2, rows, NY), lambda g: (g, 0, 0))
        return pl.BlockSpec((len(use), rows, NY), lambda g: (0, 0, 0))

    return call(
        body,
        steps,
        [pl.BlockSpec(memory_space=pltpu.SMEM)] + [block(0)] * 2 + [block(1)] * 2 + [whole((NY, NY))] * 2,
        [slot(use) for use in uses],
        [jax.ShapeDtypeStruct((len(use), rows, NY), F32) for use in uses],
        COST["rows"],
    )(voltages, source, labels, source, labels, *[jnp.asarray(part) for part in BASIS_T])


def put(out, value):
    out[...] = value


def own_part(flags, inverse, weights, table, ends, others):
    count = len(ends)
    rows = ends[0].shape[1]
    total = 2 + others[0].shape[0]

    def stack(slots, slot):
        return [pl.BlockSpec((None, rows, NY), lambda g: (jnp.clip(slot(g), 0, slots - 1), 0, 0))] * count

    def body(flag, inv_ref, wts, *refs):
        th, tl = refs[:2]
        end_refs, other_refs = refs[2:2 + count], refs[2 + count:2 + 2 * count]
        out, first_out, last_out, ring = refs[2 + 2 * count:]
        g = pl.program_id(0)

        def load(group):
            ring[lax.rem(g, 3)] = dot3(halves((th, tl)), joined(group))

        pl.when((g == 0) | (g == total - 1))(lambda: load(end_refs))
        pl.when((g > 0) & (g < total - 1))(lambda: load(other_refs))

        @pl.when(g == 0)
        def _():
            first_out[...] = ring[0]

        @pl.when(g == total - 1)
        def _():
            last_out[...] = ring[(total - 1) % 3]

        @pl.when(g > 0)
        def _():
            plane = g - 1
            bottom, top = plane == 0, plane == total - 1
            mid, inv = ring[lax.rem(plane, 3)], inv_ref[...]
            below = jnp.where(bottom, 0.0, ring[lax.rem(plane + 2, 3)])
            above = jnp.where(top, 0.0, ring[lax.rem(plane + 1, 3)])
            turn = jnp.where(bottom, flag[0], 0.0) - jnp.where(top, flag[1], 0.0)
            far = wts[:, 2:3] * (below + above) + (turn * wts[:, 4:5]) * mid
            out[...] = inv * (wts[:, 0:1] * mid + inv * far)

    return call(
        body,
        total + 1,
        [pl.BlockSpec(memory_space=pltpu.SMEM), whole((NX, NY)), whole((NX, 128))]
        + [whole((NX, NX))] * 2
        + stack(2, lambda g: jnp.where(g > 0, 1, 0))
        + stack(total - 2, lambda g: total - 2 - g),
        [
            pl.BlockSpec((None, NX, NY), lambda g: (jnp.maximum(g - 1, 0), 0, 0)),
            whole((NX, NY)),
            whole((NX, NY)),
        ],
        [
            jax.ShapeDtypeStruct((total, NX, NY), F32),
            jax.ShapeDtypeStruct((NX, NY), F32),
            jax.ShapeDtypeStruct((NX, NY), F32),
        ],
        COST["own"],
        scratch=[pltpu.VMEM((3, NX, NY), F32)],
    )(flags, inverse, weights, *table, *ends, *others)


def part_specs(parts, slot):
    return [pl.BlockSpec((None,) + part.shape[1:], lambda g: (slot, 0, 0)) for part in parts]


def first_planes(inverse, weights, x_table, outer, inner, partial, own_first, own_last, rows_table, table):
    count, total, rows = len(outer), partial.shape[0], rows_table[0].shape[0]

    def body(*refs):
        inv, wts = refs[:2]
        outer_refs, inner_refs = refs[4:4 + count], refs[4 + count:4 + 2 * count]
        part, first_ref, last_ref = refs[4 + 2 * count:7 + 2 * count]
        near_rows, grid_table = refs[7 + 2 * count:9 + 2 * count], refs[9 + 2 * count:11 + 2 * count]
        top, plane_0, plane_1, plane_2, to_above, to_below, out = refs[-7:]
        g = pl.program_id(0)

        def fill(target, group):
            target[...] = dot3(halves(refs[2:4]), joined(group))

        @pl.when(g == 0)
        def _():
            fill(top, outer_refs)
            to_above[...] = wts[:, 2:3] * last_ref[...] + wts[:, 3:4] * top[...]

        @pl.when(g == 1)
        def _():
            fill(plane_0, outer_refs)
            to_below[...] = wts[:, 2:3] * first_ref[...] + wts[:, 3:4] * plane_0[...]

        @pl.when(g == 2)
        def _():
            fill(plane_1, inner_refs)

        @pl.when(g == 3)
        def _():
            fill(plane_2, inner_refs)
            modes = part[...] + other_part(inv[...], wts, plane_0[...], plane_1[...], plane_2[...])
            out[...] = dot3(split(dot3(halves(near_rows), split(modes))), halves(grid_table))

    stack = (None,) + outer[0].shape[1:]
    return call(
        body,
        4,
        [whole((NX, NY)), whole((NX, 128))] + [whole((NX, NX))] * 2
        + [pl.BlockSpec(stack, lambda g: (jnp.minimum(g, 1), 0, 0))] * count
        + [pl.BlockSpec(stack, lambda g: (jnp.maximum(g - 2, 0), 0, 0))] * count
        + [pl.BlockSpec((None, NX, NY), lambda g: (1, 0, 0))] + [whole((NX, NY))] * 2
        + [whole((rows, NX))] * 2 + [whole((NY, NY))] * 2,
        [whole((NX, NY))] * 6 + [pl.BlockSpec((None, rows, NY), lambda g: (1, 0, 0))],
        [jax.ShapeDtypeStruct((NX, NY), F32)] * 6 + [jax.ShapeDtypeStruct((total, rows, NY), F32)],
        COST["first"],
    )(inverse, weights, *x_table, *outer, *inner, partial, own_first, own_last, *rows_table, *table)


def next_planes(inverse, weights, x_table, parts, partial, place, low, mid, rows_table, table, buffer):
    count, total, rows = len(parts), partial.shape[0], rows_table[0].shape[0]

    def body(*refs):
        inv, wts = refs[:2]
        part, low_ref, mid_ref = refs[4 + count:7 + count]
        near_rows, grid_table = refs[7 + count:9 + count], refs[9 + count:11 + count]
        high_out, higher_out, out = refs[-3:]
        g = pl.program_id(0)

        def finish(target, *planes):
            target[...] = dot3(halves(refs[2:4]), joined(refs[4:4 + count]))
            modes = part[...] + other_part(inv[...], wts, *[plane[...] for plane in planes], target[...])
            out[...] = dot3(split(dot3(halves(near_rows), split(modes))), halves(grid_table))

        pl.when(g == 0)(lambda: finish(high_out, low_ref, mid_ref))
        pl.when(g == 1)(lambda: finish(higher_out, mid_ref, high_out))

    return call(
        body,
        2,
        [whole((NX, NY)), whole((NX, 128))] + [whole((NX, NX))] * 2
        + [pl.BlockSpec((None,) + parts[0].shape[1:], lambda g: (g, 0, 0))] * count
        + [pl.BlockSpec((None, NX, NY), lambda g: (place + g, 0, 0))] + [whole((NX, NY))] * 2
        + [whole((rows, NX))] * 2 + [whole((NY, NY))] * 2 + [pl.BlockSpec(memory_space=pl.ANY)],
        [whole((NX, NY))] * 2 + [pl.BlockSpec((None, rows, NY), lambda g: (place + g, 0, 0))],
        [jax.ShapeDtypeStruct((NX, NY), F32)] * 2 + [jax.ShapeDtypeStruct((total, rows, NY), F32)],
        COST["next"],
        aliases={11 + count: 2},
    )(inverse, weights, *x_table, *parts, partial, low, mid, *rows_table, *table, buffer)


def end_plane(inverse, weights, partial, mid, high, edge, rows_table, table, buffer):
    rows = rows_table[0].shape[0]

    def body(inv_ref, wts, part, mid_ref, high_ref, edge_ref, *refs):
        inv = inv_ref[...]
        modes = part[...] + other_part(inv, wts, None, mid_ref[...], high_ref[...]) + inv * inv * edge_ref[...]
        refs[-1][...] = dot3(split(dot3(halves(refs[:2]), split(modes))), halves(refs[2:4]))

    return call(
        body,
        1,
        [whole((NX, NY)), whole((NX, 128)), pl.BlockSpec((None, NX, NY), lambda g: (0, 0, 0))]
        + [whole((NX, NY))] * 3 + [whole((rows, NX))] * 2 + [whole((NY, NY))] * 2
        + [pl.BlockSpec(memory_space=pl.ANY)],
        pl.BlockSpec((None, rows, NY), lambda g: (0, 0, 0)),
        jax.ShapeDtypeStruct(buffer.shape, F32),
        COST["step"],
        aliases={10: 0},
    )(inverse, weights, partial, mid, high, edge, *rows_table, *table, buffer)


def other_part(inv, wts, low, mid, high):
    far = low if high is None else high if low is None else low + high
    return inv * (wts[:, 1:2] * mid + inv * (wts[:, 3:4] * far))


def step(inverse, weights, x_table, parts, slot, partial, place, low, mid, rows_table, table, buffer):
    total, rows, count = partial.shape[0], rows_table[0].shape[0], len(parts)
    aliased = 0 if buffer is None else 1

    def body(*refs):
        inv, wts = refs[:2]
        part, low_ref, mid_ref = refs[4 + count:7 + count]
        near_rows, grid_table = refs[7 + count:9 + count], refs[9 + count:11 + count]
        high_out, out = refs[-2:]
        high = dot3(halves(refs[2:4]), joined(refs[4:4 + count]))
        high_out[...] = high
        modes = part[...] + other_part(inv[...], wts, low_ref[...], mid_ref[...], high)
        out[...] = dot3(split(dot3(halves(near_rows), split(modes))), halves(grid_table))

    return call(
        body,
        1,
        [whole((NX, NY)), whole((NX, 128))] + [whole((NX, NX))] * 2 + part_specs(parts, slot)
        + [pl.BlockSpec((None, NX, NY), lambda g: (place, 0, 0))] + [whole((NX, NY))] * 2
        + [whole((rows, NX))] * 2 + [whole((NY, NY))] * 2 + [pl.BlockSpec(memory_space=pl.ANY)] * aliased,
        [whole((NX, NY)), pl.BlockSpec((None, rows, NY), lambda g: (place, 0, 0))],
        [jax.ShapeDtypeStruct((NX, NY), F32), jax.ShapeDtypeStruct((total, rows, NY), F32)],
        COST["step"],
        aliases={11 + count: 1} if aliased else None,
    )(inverse, weights, *x_table, *parts, partial, low, mid, *rows_table, *table, *([buffer] if aliased else []))


def last_planes(inverse, weights, partial, x_table, parts, before, early, top, edge, rows_table, table, buffer):
    total, rows = buffer.shape[0], buffer.shape[1]
    count = len(parts)

    def body(*refs):
        inv_ref, wts, part = refs[:3]
        before_ref, early_ref, top_ref, edge_ref = refs[5 + count:9 + count]
        near_rows, grid_table = refs[9 + count:11 + count], refs[11 + count:13 + count]
        out, late = refs[-2:]
        g = pl.program_id(0)

        def finish(low, mid, high, edge=None):
            inv = inv_ref[...]
            far = wts[:, 3:4] * (low[...] if high is None else low[...] + high[...])
            if edge is not None:
                far = far + edge[...]
            modes = part[...] + inv * (wts[:, 1:2] * mid[...] + inv * far)
            out[...] = dot3(split(dot3(halves(near_rows), split(modes))), halves(grid_table))

        @pl.when(g == 0)
        def _():
            late[...] = dot3(halves(refs[3:5]), joined(refs[5:5 + count]))
            finish(before_ref, early_ref, late)

        pl.when(g == 1)(lambda: finish(early_ref, late, top_ref))
        pl.when(g == 2)(lambda: finish(late, top_ref, None, edge_ref))

    return call(
        body,
        3,
        [whole((NX, NY)), whole((NX, 128)), pl.BlockSpec((None, NX, NY), lambda g: (total - 3 + g, 0, 0))]
        + [whole((NX, NX))] * 2 + part_specs(parts, 0) + [whole((NX, NY))] * 4
        + [whole((rows, NX))] * 2 + [whole((NY, NY))] * 2 + [pl.BlockSpec(memory_space=pl.ANY)],
        pl.BlockSpec((None, rows, NY), lambda g: (total - 3 + g, 0, 0)),
        jax.ShapeDtypeStruct((total, rows, NY), F32),
        COST["last"],
        scratch=[pltpu.VMEM((NX, NY), F32)],
        aliases={13 + count: 0},
    )(inverse, weights, partial, *x_table, *parts, before, early, top, edge, *rows_table, *table, buffer)


def to_mirror(block):
    count = lax.axis_size("axial")
    return lax.ppermute(block, "axial", [(i, count - 1 - i) for i in range(count)])


def gather_rows(block):
    count = lax.axis_size("trans")
    parts = [block]
    for step in range(1, count):
        route = [(i, (i - step) % count) for i in range(count)]
        parts.append(lax.ppermute(block, "trans", route))
    return parts


def halo(first, last):
    count = lax.axis_size("axial")
    up = [(i, i + 1) for i in range(count - 1) if i + 1 != count // 2]
    below = lax.ppermute(last, "axial", up)
    above = lax.ppermute(first, "axial", [(j, i) for i, j in up])
    return below, above


def on_device(source, labels, voltages, relax):
    planes, rows = source.shape[0], source.shape[1]
    half, end = planes // 2, planes - 1
    ax_count = lax.axis_size("axial")
    position = lax.axis_index("axial")
    row_start = lax.axis_index("trans") * rows

    inner = list(range(end - 1, 0, -1))
    chunks = [[0, end], inner[:2], inner[2:4]] + [[plane] for plane in inner[4:]]
    (ends,) = row_modes(source, labels, voltages, [0, end], [[0, end]])
    others, *rest = row_modes(source, labels, after(voltages, ends), inner, [inner] + chunks[1:])
    ends, others = gather_rows(ends), gather_rows(others)
    sent = []
    for number, block in enumerate([ends[0]] + rest):
        if number < 3:
            sent.append(to_mirror(block))

    x_table = tuple(
        lax.dynamic_slice_in_dim(jnp.concatenate([part, part], axis=1), row_start, NX, 1)
        for part in (jnp.asarray(BASIS[0]), jnp.asarray(BASIS[1]))
    )
    rows_table = tuple(
        lax.dynamic_slice_in_dim(jnp.asarray(part), row_start, rows, 0) for part in BASIS_T
    )
    table = tuple(jnp.asarray(part) for part in BASIS)

    index = jnp.arange(NX, dtype=F32) + 1.0
    eigen = 2.0 - 2.0 * jnp.cos(jnp.pi * index / (NX + 1.0))
    inverse = 1.0 / (eigen[:, None] + eigen[None, :] + 2.0)
    even, odd = relax[0], relax[1]
    a_even, a_odd = (2.0 - even) * even, (2.0 - odd) * odd
    b_even, b_odd = even * even, odd * odd
    columns = [
        0.5 * (a_even + a_odd),
        0.5 * (a_even - a_odd),
        0.5 * (b_even + b_odd),
        0.5 * (b_even - b_odd),
        even * odd,
    ]
    weights = jnp.pad(jnp.stack(columns, axis=1), ((0, 0), (0, 128 - len(columns))))
    flags = jnp.stack([position == ax_count // 2, position == ax_count // 2 - 1]).astype(F32)

    passed = [gather_rows(after(sent[0], *x_table, *rows_table, inverse, weights, flags))]
    partial, own_first, own_last = own_part(flags, inverse, weights, x_table, ends, others)
    passed.append(gather_rows(sent[1]))
    sent += [to_mirror(after(block, passed[0][-1], partial)) for block in rest[2:]]
    passed.append(gather_rows(after(sent[2], partial)))
    top, plane_0, low, mid, to_above, to_below, out = first_planes(
        inverse, weights, x_table, [after(passed[0][0], sent[2])] + passed[0][1:], passed[1],
        partial, own_first, own_last, rows_table, table,
    )
    plane_1 = low
    passed.append(gather_rows(after(sent[-2], out)))
    for number in range(2, len(sent) - 2):
        low, mid, out = next_planes(
            inverse, weights, x_table, passed[number], partial, 2 * number - 2, low, mid, rows_table, table, out
        )
    below, above = halo(after(to_below, sent[-1]), after(to_above, sent[-1]))
    final = gather_rows(sent[-1])
    high, out = step(
        inverse, weights, x_table, [after(passed[-1][0], sent[-1])] + passed[-1][1:], 0,
        partial, planes - 4, low, mid, rows_table, table, out,
    )
    low, mid = mid, high
    out = end_plane(inverse, weights, partial, plane_0, plane_1, below, rows_table, table, out)
    return last_planes(
        inverse, weights, partial, x_table, final, low, mid, top, above, rows_table, table, out
    )


def solution(mesh):
    placed = (P("axial", "trans", None), P("axial", "trans", None), P(), P())
    return jax.shard_map(
        on_device, mesh=mesh, in_specs=placed, out_specs=P("axial", "trans", None), check_vma=False
    )
```

```python
import functools

import jax
import jax.numpy as jnp
import ml_dtypes
import numpy as np
from jax import lax
from jax.experimental import pallas as pl
from jax.experimental.pallas import tpu as pltpu
from jax.sharding import PartitionSpec as P

NX = 512
NY = 512
F32 = jnp.float32
BF16 = jnp.bfloat16
VMEM_LIMIT = 63 * 1024 * 1024


def table_parts():
    f = np.float32
    index = np.arange(NX, dtype=f) + f(1)
    inverse = f(1) / f(NX + 1)
    angle = ((f(np.pi) * index[:, None]) * index[None, :]) * inverse
    basis = np.sqrt(f(2) / f(NX + 1)).astype(f) * np.sin(angle.astype(np.float64)).astype(f)
    high = basis.astype(ml_dtypes.bfloat16)
    low = (basis - high.astype(f)).astype(ml_dtypes.bfloat16)
    return high, low


BASIS = table_parts()
BASIS_T = tuple(np.ascontiguousarray(part.T) for part in BASIS)


def split(x):
    high = x.astype(BF16)
    return high, (x - high.astype(F32)).astype(BF16)


def dot3(left, right):
    def dot(a, b):
        return jnp.dot(a, b, preferred_element_type=F32)

    return dot(left[0], right[0]) + (dot(left[0], right[1]) + dot(left[1], right[0]))


def after(value, *others):
    return lax.optimization_barrier((value,) + others)[0]


def whole(shape):
    return pl.BlockSpec(shape, lambda g: (0,) * len(shape))


def call(body, grid, in_specs, out_specs, out_shape, cost, scratch=(), aliases=None):
    return pl.pallas_call(
        body,
        grid=(grid,),
        in_specs=in_specs,
        out_specs=out_specs,
        out_shape=out_shape,
        scratch_shapes=scratch,
        input_output_aliases=aliases or {},
        compiler_params=pltpu.CompilerParams(
            dimension_semantics=("arbitrary",), vmem_limit_bytes=VMEM_LIMIT
        ),
        cost_estimate=pl.CostEstimate(flops=cost[0], bytes_accessed=cost[1], transcendentals=0),
    )


COST = {
    "rows": (1, 1),
    "modes": (1, 1),
    "own": (1, 1),
    "first": (1, 1),
    "next": (1, 1),
    "step": (1, 1),
    "base": (1, 1),
    "last": (1, 1),
}


def halves(refs):
    return tuple(ref[...] for ref in refs)


def joined(refs):
    return split(jnp.concatenate([ref[...] for ref in refs], axis=0))


def row_modes(source, labels, voltages, planes, uses):
    rows = source.shape[1]
    steps = len(planes) // 2

    def body(volts, *refs):
        high, low = refs[4:6]
        charge = []
        for source_ref, labels_ref in (refs[0:2], refs[2:4]):
            label = labels_ref[...]
            pick = jnp.full(label.shape, volts[0], F32)
            for region in range(1, volts.shape[0]):
                pick = jnp.where(label == region, volts[region], pick)
            charge.append(source_ref[...] + pick)
        modes = dot3(split(jnp.concatenate(charge, axis=0)), (high[...], low[...]))
        modes = modes.reshape(2, rows, NY)
        g = pl.program_id(0)
        for use, out in zip(uses, refs[6:]):
            start = planes.index(use[0])
            if len(use) == len(planes):
                out[...] = modes
            else:
                part = modes if len(use) == 2 else modes[start % 2:start % 2 + 1]
                pl.when(g == start // 2)(functools.partial(put, out, part))

    def block(which):
        if steps == 1:
            return pl.BlockSpec((None, rows, NY), lambda g: (planes[which], 0, 0))
        return pl.BlockSpec((None, rows, NY), lambda g: (planes[which] - 2 * g, 0, 0))

    def slot(use):
        if len(use) == len(planes):
            return pl.BlockSpec((2, rows, NY), lambda g: (g, 0, 0))
        return pl.BlockSpec((len(use), rows, NY), lambda g: (0, 0, 0))

    return call(
        body,
        steps,
        [pl.BlockSpec(memory_space=pltpu.SMEM)] + [block(0)] * 2 + [block(1)] * 2 + [whole((NY, NY))] * 2,
        [slot(use) for use in uses],
        [jax.ShapeDtypeStruct((len(use), rows, NY), F32) for use in uses],
        COST["rows"],
    )(voltages, source, labels, source, labels, *[jnp.asarray(part) for part in BASIS_T])


def put(out, value):
    out[...] = value


def own_part(flags, inverse, weights, table, ends, others):
    count = len(ends)
    rows = ends[0].shape[1]
    total = 2 + others[0].shape[0]

    def stack(slots, slot):
        return [pl.BlockSpec((None, rows, NY), lambda g: (jnp.clip(slot(g), 0, slots - 1), 0, 0))] * count

    def body(flag, inv_ref, wts, *refs):
        th, tl = refs[:2]
        end_refs, other_refs = refs[2:2 + count], refs[2 + count:2 + 2 * count]
        out, first_out, last_out, ring = refs[2 + 2 * count:]
        g = pl.program_id(0)

        def load(group):
            ring[lax.rem(g, 3)] = dot3(halves((th, tl)), joined(group))

        pl.when((g == 0) | (g == total - 1))(lambda: load(end_refs))
        pl.when((g > 0) & (g < total - 1))(lambda: load(other_refs))

        @pl.when(g == 0)
        def _():
            first_out[...] = ring[0]

        @pl.when(g == total - 1)
        def _():
            last_out[...] = ring[(total - 1) % 3]

        @pl.when(g > 0)
        def _():
            plane = g - 1
            bottom, top = plane == 0, plane == total - 1
            mid, inv = ring[lax.rem(plane, 3)], inv_ref[...]
            below = jnp.where(bottom, 0.0, ring[lax.rem(plane + 2, 3)])
            above = jnp.where(top, 0.0, ring[lax.rem(plane + 1, 3)])
            turn = jnp.where(bottom, flag[0], 0.0) - jnp.where(top, flag[1], 0.0)
            far = wts[:, 2:3] * (below + above) + (turn * wts[:, 4:5]) * mid
            out[...] = inv * (wts[:, 0:1] * mid + inv * far)

    return call(
        body,
        total + 1,
        [pl.BlockSpec(memory_space=pltpu.SMEM), whole((NX, NY)), whole((NX, 128))]
        + [whole((NX, NX))] * 2
        + stack(2, lambda g: jnp.where(g > 0, 1, 0))
        + stack(total - 2, lambda g: total - 2 - g),
        [
            pl.BlockSpec((None, NX, NY), lambda g: (jnp.maximum(g - 1, 0), 0, 0)),
            whole((NX, NY)),
            whole((NX, NY)),
        ],
        [
            jax.ShapeDtypeStruct((total, NX, NY), F32),
            jax.ShapeDtypeStruct((NX, NY), F32),
            jax.ShapeDtypeStruct((NX, NY), F32),
        ],
        COST["own"],
        scratch=[pltpu.VMEM((3, NX, NY), F32)],
    )(flags, inverse, weights, *table, *ends, *others)


def part_specs(parts, slot):
    return [pl.BlockSpec((None,) + part.shape[1:], lambda g: (slot, 0, 0)) for part in parts]


def first_planes(inverse, weights, x_table, outer, inner, partial, own_first, own_last, rows_table, table):
    count, total, rows = len(outer), partial.shape[0], rows_table[0].shape[0]

    def body(*refs):
        inv, wts = refs[:2]
        outer_refs, inner_refs = refs[4:4 + count], refs[4 + count:4 + 2 * count]
        part, first_ref, last_ref = refs[4 + 2 * count:7 + 2 * count]
        near_rows, grid_table = refs[7 + 2 * count:9 + 2 * count], refs[9 + 2 * count:11 + 2 * count]
        top, plane_0, plane_1, plane_2, to_above, to_below, out = refs[-7:]
        g = pl.program_id(0)

        def fill(target, group):
            target[...] = dot3(halves(refs[2:4]), joined(group))

        @pl.when(g == 0)
        def _():
            fill(top, outer_refs)
            to_above[...] = wts[:, 2:3] * last_ref[...] + wts[:, 3:4] * top[...]

        @pl.when(g == 1)
        def _():
            fill(plane_0, outer_refs)
            to_below[...] = wts[:, 2:3] * first_ref[...] + wts[:, 3:4] * plane_0[...]

        @pl.when(g == 2)
        def _():
            fill(plane_1, inner_refs)

        @pl.when(g == 3)
        def _():
            fill(plane_2, inner_refs)
            modes = part[...] + other_part(inv[...], wts, plane_0[...], plane_1[...], plane_2[...])
            out[...] = dot3(split(dot3(halves(near_rows), split(modes))), halves(grid_table))

    stack = (None,) + outer[0].shape[1:]
    return call(
        body,
        4,
        [whole((NX, NY)), whole((NX, 128))] + [whole((NX, NX))] * 2
        + [pl.BlockSpec(stack, lambda g: (jnp.minimum(g, 1), 0, 0))] * count
        + [pl.BlockSpec(stack, lambda g: (jnp.maximum(g - 2, 0), 0, 0))] * count
        + [pl.BlockSpec((None, NX, NY), lambda g: (1, 0, 0))] + [whole((NX, NY))] * 2
        + [whole((rows, NX))] * 2 + [whole((NY, NY))] * 2,
        [whole((NX, NY))] * 6 + [pl.BlockSpec((None, rows, NY), lambda g: (1, 0, 0))],
        [jax.ShapeDtypeStruct((NX, NY), F32)] * 6 + [jax.ShapeDtypeStruct((total, rows, NY), F32)],
        COST["first"],
    )(inverse, weights, *x_table, *outer, *inner, partial, own_first, own_last, *rows_table, *table)


def next_planes(inverse, weights, x_table, parts, partial, place, low, mid, rows_table, table, buffer):
    count, total, rows = len(parts), partial.shape[0], rows_table[0].shape[0]

    def body(*refs):
        inv, wts = refs[:2]
        part, low_ref, mid_ref = refs[4 + count:7 + count]
        near_rows, grid_table = refs[7 + count:9 + count], refs[9 + count:11 + count]
        high_out, higher_out, out = refs[-3:]
        g = pl.program_id(0)

        def finish(target, *planes):
            target[...] = dot3(halves(refs[2:4]), joined(refs[4:4 + count]))
            modes = part[...] + other_part(inv[...], wts, *[plane[...] for plane in planes], target[...])
            out[...] = dot3(split(dot3(halves(near_rows), split(modes))), halves(grid_table))

        pl.when(g == 0)(lambda: finish(high_out, low_ref, mid_ref))
        pl.when(g == 1)(lambda: finish(higher_out, mid_ref, high_out))

    return call(
        body,
        2,
        [whole((NX, NY)), whole((NX, 128))] + [whole((NX, NX))] * 2
        + [pl.BlockSpec((None,) + parts[0].shape[1:], lambda g: (g, 0, 0))] * count
        + [pl.BlockSpec((None, NX, NY), lambda g: (place + g, 0, 0))] + [whole((NX, NY))] * 2
        + [whole((rows, NX))] * 2 + [whole((NY, NY))] * 2 + [pl.BlockSpec(memory_space=pl.ANY)],
        [whole((NX, NY))] * 2 + [pl.BlockSpec((None, rows, NY), lambda g: (place + g, 0, 0))],
        [jax.ShapeDtypeStruct((NX, NY), F32)] * 2 + [jax.ShapeDtypeStruct((total, rows, NY), F32)],
        COST["next"],
        aliases={11 + count: 2},
    )(inverse, weights, *x_table, *parts, partial, low, mid, *rows_table, *table, buffer)


def end_plane(inverse, weights, partial, mid, high, edge, rows_table, table, buffer):
    rows = rows_table[0].shape[0]

    def body(inv_ref, wts, part, mid_ref, high_ref, edge_ref, *refs):
        inv = inv_ref[...]
        modes = part[...] + other_part(inv, wts, None, mid_ref[...], high_ref[...]) + inv * inv * edge_ref[...]
        refs[-1][...] = dot3(split(dot3(halves(refs[:2]), split(modes))), halves(refs[2:4]))

    return call(
        body,
        1,
        [whole((NX, NY)), whole((NX, 128)), pl.BlockSpec((None, NX, NY), lambda g: (0, 0, 0))]
        + [whole((NX, NY))] * 3 + [whole((rows, NX))] * 2 + [whole((NY, NY))] * 2
        + [pl.BlockSpec(memory_space=pl.ANY)],
        pl.BlockSpec((None, rows, NY), lambda g: (0, 0, 0)),
        jax.ShapeDtypeStruct(buffer.shape, F32),
        COST["step"],
        aliases={10: 0},
    )(inverse, weights, partial, mid, high, edge, *rows_table, *table, buffer)


def other_part(inv, wts, low, mid, high):
    far = low if high is None else high if low is None else low + high
    return inv * (wts[:, 1:2] * mid + inv * (wts[:, 3:4] * far))


def step(inverse, weights, x_table, parts, slot, partial, place, low, mid, rows_table, table, buffer):
    total, rows, count = partial.shape[0], rows_table[0].shape[0], len(parts)
    aliased = 0 if buffer is None else 1

    def body(*refs):
        inv, wts = refs[:2]
        part, low_ref, mid_ref = refs[4 + count:7 + count]
        near_rows, grid_table = refs[7 + count:9 + count], refs[9 + count:11 + count]
        high_out, out = refs[-2:]
        high = dot3(halves(refs[2:4]), joined(refs[4:4 + count]))
        high_out[...] = high
        modes = part[...] + other_part(inv[...], wts, low_ref[...], mid_ref[...], high)
        out[...] = dot3(split(dot3(halves(near_rows), split(modes))), halves(grid_table))

    return call(
        body,
        1,
        [whole((NX, NY)), whole((NX, 128))] + [whole((NX, NX))] * 2 + part_specs(parts, slot)
        + [pl.BlockSpec((None, NX, NY), lambda g: (place, 0, 0))] + [whole((NX, NY))] * 2
        + [whole((rows, NX))] * 2 + [whole((NY, NY))] * 2 + [pl.BlockSpec(memory_space=pl.ANY)] * aliased,
        [whole((NX, NY)), pl.BlockSpec((None, rows, NY), lambda g: (place, 0, 0))],
        [jax.ShapeDtypeStruct((NX, NY), F32), jax.ShapeDtypeStruct((total, rows, NY), F32)],
        COST["step"],
        aliases={11 + count: 1} if aliased else None,
    )(inverse, weights, *x_table, *parts, partial, low, mid, *rows_table, *table, *([buffer] if aliased else []))


def last_planes(inverse, weights, partial, x_table, parts, before, early, top, edge, rows_table, table, buffer):
    total, rows = buffer.shape[0], buffer.shape[1]
    count = len(parts)

    def body(*refs):
        inv_ref, wts, part = refs[:3]
        before_ref, early_ref, top_ref, edge_ref = refs[5 + count:9 + count]
        near_rows, grid_table = refs[9 + count:11 + count], refs[11 + count:13 + count]
        out, late = refs[-2:]
        g = pl.program_id(0)

        def finish(low, mid, high, edge=None):
            inv = inv_ref[...]
            far = wts[:, 3:4] * (low[...] if high is None else low[...] + high[...])
            if edge is not None:
                far = far + edge[...]
            modes = part[...] + inv * (wts[:, 1:2] * mid[...] + inv * far)
            out[...] = dot3(split(dot3(halves(near_rows), split(modes))), halves(grid_table))

        @pl.when(g == 0)
        def _():
            late[...] = dot3(halves(refs[3:5]), joined(refs[5:5 + count]))
            finish(before_ref, early_ref, late)

        pl.when(g == 1)(lambda: finish(early_ref, late, top_ref))
        pl.when(g == 2)(lambda: finish(late, top_ref, None, edge_ref))

    return call(
        body,
        3,
        [whole((NX, NY)), whole((NX, 128)), pl.BlockSpec((None, NX, NY), lambda g: (total - 3 + g, 0, 0))]
        + [whole((NX, NX))] * 2 + part_specs(parts, 0) + [whole((NX, NY))] * 4
        + [whole((rows, NX))] * 2 + [whole((NY, NY))] * 2 + [pl.BlockSpec(memory_space=pl.ANY)],
        pl.BlockSpec((None, rows, NY), lambda g: (total - 3 + g, 0, 0)),
        jax.ShapeDtypeStruct((total, rows, NY), F32),
        COST["last"],
        scratch=[pltpu.VMEM((NX, NY), F32)],
        aliases={13 + count: 0},
    )(inverse, weights, partial, *x_table, *parts, before, early, top, edge, *rows_table, *table, buffer)


def to_mirror(block):
    count = lax.axis_size("axial")
    return lax.ppermute(block, "axial", [(i, count - 1 - i) for i in range(count)])


def gather_rows(block):
    count = lax.axis_size("trans")
    parts = [block]
    for step in range(1, count):
        route = [(i, (i - step) % count) for i in range(count)]
        parts.append(lax.ppermute(block, "trans", route))
    return parts


def halo(first, last):
    count = lax.axis_size("axial")
    up = [(i, i + 1) for i in range(count - 1) if i + 1 != count // 2]
    below = lax.ppermute(last, "axial", up)
    above = lax.ppermute(first, "axial", [(j, i) for i, j in up])
    return below, above


def on_device(source, labels, voltages, relax):
    planes, rows = source.shape[0], source.shape[1]
    half, end = planes // 2, planes - 1
    ax_count = lax.axis_size("axial")
    position = lax.axis_index("axial")
    row_start = lax.axis_index("trans") * rows

    inner = list(range(end - 1, 0, -1))
    chunks = [[0, end], inner[:2], inner[2:4]] + [[plane] for plane in inner[4:]]
    (ends,) = row_modes(source, labels, voltages, [0, end], [[0, end]])
    others, *rest = row_modes(source, labels, after(voltages, ends), inner, [inner] + chunks[1:])
    ends, others = gather_rows(ends), gather_rows(others)
    sent = []
    for number, block in enumerate([ends[0]] + rest):
        if number < 3:
            sent.append(to_mirror(block))

    x_table = tuple(
        lax.dynamic_slice_in_dim(jnp.concatenate([part, part], axis=1), row_start, NX, 1)
        for part in (jnp.asarray(BASIS[0]), jnp.asarray(BASIS[1]))
    )
    rows_table = tuple(
        lax.dynamic_slice_in_dim(jnp.asarray(part), row_start, rows, 0) for part in BASIS_T
    )
    table = tuple(jnp.asarray(part) for part in BASIS)

    index = jnp.arange(NX, dtype=F32) + 1.0
    eigen = 2.0 - 2.0 * jnp.cos(jnp.pi * index / (NX + 1.0))
    inverse = 1.0 / (eigen[:, None] + eigen[None, :] + 2.0)
    even, odd = relax[0], relax[1]
    a_even, a_odd = (2.0 - even) * even, (2.0 - odd) * odd
    b_even, b_odd = even * even, odd * odd
    columns = [
        0.5 * (a_even + a_odd),
        0.5 * (a_even - a_odd),
        0.5 * (b_even + b_odd),
        0.5 * (b_even - b_odd),
        even * odd,
    ]
    weights = jnp.pad(jnp.stack(columns, axis=1), ((0, 0), (0, 128 - len(columns))))
    flags = jnp.stack([position == ax_count // 2, position == ax_count // 2 - 1]).astype(F32)

    passed = [gather_rows(after(sent[0], *x_table, *rows_table, inverse, weights, flags))]
    partial, own_first, own_last = own_part(flags, inverse, weights, x_table, ends, others)
    passed.append(gather_rows(sent[1]))
    sent += [to_mirror(after(block, passed[0][-1], partial)) for block in rest[2:]]
    passed.append(gather_rows(after(sent[2], partial)))
    top, plane_0, low, mid, to_above, to_below, out = first_planes(
        inverse, weights, x_table, [after(passed[0][0], sent[2])] + passed[0][1:], passed[1],
        partial, own_first, own_last, rows_table, table,
    )
    plane_1 = low
    passed.append(gather_rows(after(sent[-2], out)))
    for number in range(2, len(sent) - 2):
        low, mid, out = next_planes(
            inverse, weights, x_table, passed[number], partial, 2 * number - 2, low, mid, rows_table, table, out
        )
    below, above = halo(after(to_below, sent[-1]), after(to_above, sent[-1]))
    final = gather_rows(sent[-1])
    high, out = step(
        inverse, weights, x_table, [after(passed[-1][0], sent[-1])] + passed[-1][1:], 0,
        partial, planes - 4, low, mid, rows_table, table, out,
    )
    low, mid = mid, high
    out = end_plane(inverse, weights, partial, plane_0, plane_1, below, rows_table, table, out)
    return last_planes(
        inverse, weights, partial, x_table, final, low, mid, top, above, rows_table, table, out
    )


def solution(mesh):
    placed = (P("axial", "trans", None), P("axial", "trans", None), P(), P())
    return jax.shard_map(
        on_device, mesh=mesh, in_specs=placed, out_specs=P("axial", "trans", None), check_vma=False
    )
```
